32 devices in a mesh: groups: 2 (over x), vel: 16 (over z, y, core).
Axes of the slice: x: 2, y: 2, z: 4, core: 2. Of those that a mesh axis runs over, the one named last changes fastest.
Arguments:
- signal: bfloat16 [32, 8, 512], P(('groups', 'vel')), parts along dimension 0, may hold values from -6 to 6
- weight: bfloat16 [32, 8, 512], P(('groups', 'vel')), parts along dimension 0, may hold values from 0.25 to 4
- shifts: int32 [16, 16, 2], P('vel'), may hold values from -15 to 15, as said below
- phases: int32 [16, 16, 2], P('vel'), may hold values from 0 to 7, as said below
Outputs:
- likelihood: float32 [32, 8, 512], P(('groups', 'vel')), parts along dimension 0
- best_likelihood: float32 [16, 512], P('groups'), parts along dimension 0
The draws below stay inside these ranges and needn't reach their ends.
There are 2 independent parts, one for each index of `groups`. The reference program is written for one: setup_inputs(seed, part) draws one part's arguments, and reference() takes and returns one part's arrays. A program takes and returns all parts, laid end to end along the dimension named above; an argument that names none is the same for every part. Nothing has to cross between parts.
Inputs may be any that keep to these rules, and one draw needn't show every extreme that they name: shifts[v, e] = floor(o / 8) of offsets o in eighths of a pixel that grow with the exposure index e for each velocity: column offset a_v e with a_v in -8..8, row offset floor(b_v e / 16) with b_v in -8..8; some velocity has a_v = 8 and another a_v = -8. phases[v, e] = the same offsets modulo 8.
All inputs are finite; a program needn't handle non-finite values.
Results may differ from the reference program's by a relative error of at most 0.0003.
Values may be sent and summed in bfloat16 or wider, within the bound.
A program may use at most 64 MiB of HBM per device.

```python
import math
import jax
import jax.numpy as jnp
from jax import lax

H = 8
W = 512
E = 16
V = 16


def motion(key):
    base = jax.random.fold_in(key, 7)
    col_rate = jax.random.randint(jax.random.fold_in(base, 1), (V,), -8, 9, dtype=jnp.int32)
    col_rate = col_rate.at[0].set(8).at[1].set(-8).at[2].set(1)
    row_rate = jax.random.randint(jax.random.fold_in(base, 2), (V,), -8, 9, dtype=jnp.int32)
    epochs = jnp.arange(E, dtype=jnp.int32)
    col_offset = col_rate[:, None] * epochs[None, :]
    row_offset = row_rate[:, None] * epochs[None, :] // 16
    return jnp.stack([row_offset, col_offset], axis=2).astype(jnp.int32)


def draw_shifts(key, part):
    return motion(key) // 8


def draw_phases(key, part):
    return motion(key) % 8


def block_levels(stream_key, extent, split, low, high):
    def one(axis_at, parts):
        heights = jax.random.uniform(jax.random.fold_in(jax.random.fold_in(stream_key, 6), axis_at), (parts,), jnp.float32, low / len(split), high / len(split))
        return jnp.repeat(jnp.exp(heights), extent[axis_at] // parts).reshape((-1,) + (1,) * (len(extent) - axis_at - 1))

    gain = one(*split[0])
    for cut in split[1:]:
        gain = gain * one(*cut)
    return gain


def gaussian(own_key, extent, scale, most, cuts=(), kind=jnp.bfloat16):
    values = scale * jax.random.normal(own_key, extent, jnp.float32)
    if cuts:
        values = values * block_levels(own_key, extent, cuts, -0.22, 0.18)
    return jnp.clip(values, -most, most).astype(kind)


def setup_inputs(seed: int = 0, part: int = 0) -> dict:
    arg_keys = jax.random.split(jax.random.key(seed), 5)
    part_splits = jax.random.split(jax.random.fold_in(arg_keys[4], part), 5)
    return {
        "signal": gaussian(part_splits[0], (E, H, W), 1.0, 6.0, ((0, 16),)),
        "weight": jnp.clip(jnp.exp(math.log(4.0) - 2.7725887 * jax.random.uniform(part_splits[1], (E, H, W), jnp.float32) ** block_levels(part_splits[1], (E, H, W), ((0, 16),), -0.2, 0.2)), 0.25, 4.0).astype(jnp.bfloat16),
        "shifts": draw_shifts(jax.random.fold_in(arg_keys[4], 71), part),
        "phases": draw_phases(jax.random.fold_in(arg_keys[4], 71), part),
    }


def tap_table():
    fraction = jnp.arange(8, dtype=jnp.float32) / 8.0
    position = (jnp.arange(6, dtype=jnp.int32) - 2).astype(jnp.float32)
    distance = position[None, :] - fraction[:, None]
    raw_taps = jnp.sinc(distance) * jnp.sinc(distance / 3.0)
    return (raw_taps / lax.optimization_barrier(jnp.sum(raw_taps, axis=1, keepdims=True))).astype(jnp.float32)

def pick_taps(coefficients, phase_index):
    choose = (jnp.arange(coefficients.shape[0], dtype=jnp.int32) == phase_index).astype(jnp.float32)
    return lax.optimization_barrier(jnp.sum(choose[:, None] * coefficients, axis=0))

def place_pair(padded, shift_pair, phase_pair, coefficients, margin, columns, reach):
    height = padded.shape[1]
    col_taps = pick_taps(coefficients, phase_pair[1])
    row_taps = pick_taps(coefficients, phase_pair[0])
    anchor = (shift_pair[0] * 0).astype(jnp.int32)
    col_start = (reach + shift_pair[1] - 2).astype(jnp.int32)
    slab = lax.dynamic_slice(padded, (anchor, anchor, col_start), (2, height, columns + 5)).astype(jnp.float32)
    row_pass = sum((col_taps[tap_index] * slab[:, :, tap_index:tap_index + columns] for tap_index in range(6)))
    tall = jnp.pad(row_pass, ((0, 0), (margin, margin), (0, 0)))
    row_start = (margin + shift_pair[0] - 2).astype(jnp.int32)
    slab_rows = lax.dynamic_slice(tall, (anchor, row_start, anchor), (2, height + 5, columns))
    return sum((row_taps[tap_index] * slab_rows[:, tap_index:tap_index + height, :] for tap_index in range(6)))

def place_block(padded, shift_block, phase_block, coefficients, margin, columns, reach):
    placed = jax.vmap(lambda image, shift_pair, phase_pair: place_pair(image, shift_pair, phase_pair, coefficients, margin, columns, reach))(padded, shift_block, phase_block)
    return lax.optimization_barrier(jnp.sum(placed, axis=0))

def stack_velocities(padded, shift_rows, phase_rows, coefficients, margin, columns, reach):
    count = padded.shape[0]
    height = padded.shape[2]
    block = 32 if count % 32 == 0 else count
    groups_count = count // block

    def one_velocity(inputs):
        shift_set, phase_set = inputs
        if groups_count == 1:
            return place_block(padded, shift_set, phase_set, coefficients, margin, columns, reach)
        blocked = padded.reshape((groups_count, block) + padded.shape[1:])
        shift_blocks = shift_set.reshape((groups_count, block, 2))
        phase_blocks = phase_set.reshape((groups_count, block, 2))

        def add_block(total, item):
            images, shift_block, phase_block = item
            return (total + place_block(images, shift_block, phase_block, coefficients, margin, columns, reach), None)
        start = jnp.zeros((2, height, columns), jnp.float32)
        total, unused = lax.scan(add_block, start, (blocked, shift_blocks, phase_blocks))
        return total
    return lax.map(one_velocity, (shift_rows, phase_rows))

def reference(signal, weight, shifts, phases):
    coefficients = tap_table()
    columns = signal.shape[2]
    margin = shifts.shape[1] // 16 + 6
    reach = shifts.shape[1] + 3
    images = jnp.stack([signal, weight], axis=1)
    padded = jnp.pad(images, ((0, 0), (0, 0), (0, 0), (reach, reach)))
    summed = stack_velocities(padded, shifts, phases, coefficients, margin, columns, reach)
    likelihood = summed[:, 0] / jnp.sqrt(jnp.maximum(summed[:, 1], 1.0))
    best_likelihood = lax.optimization_barrier(jnp.max(likelihood, axis=0))
    return (likelihood, best_likelihood)
```

```python
import functools
import math

import jax
import jax.numpy as jnp
import numpy as np
from jax import lax
from jax.experimental import pallas as pl
from jax.experimental.pallas import tpu as pltpu
from jax.sharding import PartitionSpec as P

TAPS = 6
PHASES = 8
LANES = 128
MESH = pl.DeviceIdType.MESH


def tap_table():
    distance = (np.arange(TAPS)[None, :] - 2) - np.arange(PHASES)[:, None] / 8.0
    raw = np.sinc(distance) * np.sinc(distance / 3.0)
    return (raw / raw.sum(axis=1, keepdims=True)).astype(np.float32)


def loop(start, stop, step):
    if stop - start <= 16:
        for at in range(start, stop):
            step(at)
    else:
        lax.fori_loop(start, stop, lambda at, c: (step(at), c)[1], 0)


def pick_phase(phase, column):
    value = jnp.full(phase.shape, float(column[0]), jnp.float32)
    for at in range(1, PHASES):
        value = jnp.where(phase == at, float(column[at]), value)
    return value


def coefficient_rows(shifts_ref, phases_ref, exposures, height):
    depth = exposures * 2 * height
    table = tap_table()
    lane = lax.broadcasted_iota(jnp.int32, (1, depth), 1)
    owner = lane // (2 * height)

    def spread(e, held):
        row_shift, row_phase, col_phase = held
        here = owner == e
        return (
            jnp.where(here, shifts_ref[0, e, 0], row_shift),
            jnp.where(here, phases_ref[0, e, 0], row_phase),
            jnp.where(here, phases_ref[0, e, 1], col_phase),
        )

    held = (jnp.zeros((1, depth), jnp.int32),) * 3
    if exposures <= 16:
        for e in range(exposures):
            held = spread(e, held)
    else:
        held = lax.fori_loop(0, exposures, spread, held)
    row_shift, row_phase, col_phase = held
    row_out = lax.broadcasted_iota(jnp.int32, (height, depth), 0)
    tap_index = lane % height - row_out + 2 - row_shift
    row_taps = jnp.zeros((height, depth), jnp.float32)
    for k in range(TAPS):
        row_taps = jnp.where(tap_index == k, pick_phase(row_phase, table[:, k]), row_taps)
    col_taps = [pick_phase(col_phase, table[:, k]) for k in range(TAPS)]
    image = (lane // height) % 2
    rows = []
    for which in range(2):
        masked = jnp.where(image == which, row_taps, 0.0)
        rows += [masked * col_taps[k] for k in range(TAPS)]
    full = jnp.concatenate(rows, axis=0)
    high = full.astype(jnp.bfloat16)
    low = (full - high.astype(jnp.float32)).astype(jnp.bfloat16)
    return jnp.concatenate([high, low], axis=0)


def kernel(
    count, height, columns, wide, owners, rows,
    signal_ref, weight_ref, shifts_ref, phases_ref, lik_ref, best_ref,
    images, moved, coefs, chunks, partial, final,
    send_a, send_f, recv_a, send_r, recv_r, send_g, recv_g,
):
    me = lax.axis_index("vel")
    core = lax.rem(me, 2)
    chip = me // 2
    chips = count // 2
    partner = me + 1 - 2 * core

    barrier = pltpu.get_barrier_semaphore()

    def greet(d):
        pl.semaphore_signal(
            barrier, inc=1, device_id={"vel": lax.rem(me + d, count)}, device_id_type=MESH
        )

    loop(1, count, greet)
    images[me] = jnp.concatenate(
        [signal_ref[0].astype(jnp.float32), weight_ref[0].astype(jnp.float32)], axis=0
    ).astype(jnp.bfloat16)
    coefs[...] = coefficient_rows(shifts_ref, phases_ref, count, height)
    pl.semaphore_wait(barrier, count - 1)

    def block_copy(e, to, send_sem):
        return pltpu.make_async_remote_copy(
            src_ref=images.at[e], dst_ref=images.at[e], send_sem=send_sem,
            recv_sem=recv_a.at[e], device_id={"vel": to}, device_id_type=MESH,
        )

    def source(d, side):
        return lax.rem(chip + chips - d, chips) * 2 + side

    def target(d):
        return lax.rem(chip + d, chips) * 2 + core

    def place(e):
        block = images[e].astype(jnp.float32)
        block = jnp.concatenate(
            [block, jnp.zeros((2 * height, wide - columns), jnp.float32)], axis=1
        )
        amount = lax.rem(wide + 2 - shifts_ref[0, e, 1], wide)
        start = pl.multiple_of(e * 2 * height, 2 * height)
        moved[pl.ds(start, 2 * height), :] = pltpu.roll(block, amount, 1).astype(jnp.bfloat16)

    loop(1, chips, lambda d: block_copy(me, target(d), send_a.at[d]).start())
    block_copy(me, partner, send_f.at[0]).start()
    place(me)

    def relay(d):
        e = source(d, core)
        block_copy(e, partner, send_f.at[d]).wait_recv()
        block_copy(e, partner, send_f.at[d]).start()
        place(e)

    loop(1, chips, relay)

    def arrive(d):
        e = source(d, 1 - core)
        block_copy(e, partner, send_f.at[d]).wait_recv()
        place(e)

    loop(0, chips, arrive)

    acc = jnp.dot(coefs[...], moved[...], preferred_element_type=jnp.float32)
    half = 2 * TAPS * height
    acc = acc[:half] + acc[half:]
    sums = []
    for which in range(2):
        total = None
        for k in range(TAPS):
            at = (which * TAPS + k) * height
            term = acc[at : at + height]
            if k:
                term = pltpu.roll(term, wide - k, 1)
            term = term[:, :columns]
            total = term if total is None else total + term
        sums.append(total)
    likelihood = sums[0] / jnp.sqrt(jnp.maximum(sums[1], 1.0))
    lik_ref[0] = likelihood

    tiles = columns // LANES
    per_tile = height // rows
    for tile in range(tiles):
        for part in range(per_tile):
            chunks[tile * per_tile + part] = likelihood[
                part * rows : (part + 1) * rows, tile * LANES : (tile + 1) * LANES
            ]

    def chunk_copy(owner, slot, to):
        return pltpu.make_async_remote_copy(
            src_ref=chunks.at[owner], dst_ref=partial.at[slot], send_sem=send_r.at[owner],
            recv_sem=recv_r.at[slot], device_id={"vel": to}, device_id_type=MESH,
        )

    def final_copy(slot, to, send_sem):
        return pltpu.make_async_remote_copy(
            src_ref=final.at[slot], dst_ref=final.at[slot], send_sem=send_sem,
            recv_sem=recv_g.at[slot], device_id={"vel": to}, device_id_type=MESH,
        )

    whole_group = owners == count

    def send_chunk(d):
        to = lax.rem(me + d, count)
        if whole_group:
            chunk_copy(to, me, to).start()
        else:
            @pl.when(to < owners)
            def _():
                chunk_copy(to, me, to).start()

    loop(1, count, send_chunk)

    def reduce_own():
        partial[me] = chunks[me]
        loop(1, count, lambda d: chunk_copy(me, lax.rem(me + d, count), me).wait_recv())
        final[me] = jnp.max(partial[...], axis=0)
        loop(
            1, count,
            lambda d: final_copy(me, lax.rem(me + d, count), send_g.at[d]).start(),
        )

    if whole_group:
        reduce_own()
    else:
        pl.when(me < owners)(reduce_own)

    def take_final(d):
        slot = lax.rem(me + count - d, count)
        if whole_group:
            final_copy(slot, partner, send_g.at[d]).wait_recv()
        else:
            @pl.when(slot < owners)
            def _():
                final_copy(slot, partner, send_g.at[d]).wait_recv()

    loop(1, count, take_final)
    for tile in range(tiles):
        for part in range(per_tile):
            best_ref[part * rows : (part + 1) * rows, tile * LANES : (tile + 1) * LANES] = final[
                tile * per_tile + part
            ]

    loop(1, chips, lambda d: block_copy(me, target(d), send_a.at[d]).wait_send())
    loop(0, chips, lambda d: block_copy(source(d, core), partner, send_f.at[d]).wait_send())

    def sent_chunk(d):
        to = lax.rem(me + d, count)
        if whole_group:
            chunk_copy(to, me, to).wait_send()
        else:
            @pl.when(to < owners)
            def _():
                chunk_copy(to, me, to).wait_send()

    loop(1, count, sent_chunk)

    def sent_final():
        loop(
            1, count,
            lambda d: final_copy(me, lax.rem(me + d, count), send_g.at[d]).wait_send(),
        )

    if whole_group:
        sent_final()
    else:
        pl.when(me < owners)(sent_final)


def body(count, signal, weight, shifts, phases):
    height, columns = signal.shape[1], signal.shape[2]
    reach = shifts.shape[1] + 5
    wide = columns + -(-reach // LANES) * LANES
    pieces = height * columns // LANES
    rows = max(1, pieces // count)
    owners = pieces // rows
    dma = pltpu.SemaphoreType.DMA
    vmem = pl.BlockSpec(memory_space=pltpu.VMEM)
    smem = pl.BlockSpec(memory_space=pltpu.SMEM)
    return pl.pallas_call(
        functools.partial(kernel, count, height, columns, wide, owners, rows),
        out_shape=(
            jax.ShapeDtypeStruct((1, height, columns), jnp.float32),
            jax.ShapeDtypeStruct((height, columns), jnp.float32),
        ),
        in_specs=[vmem, vmem, smem, smem],
        out_specs=(vmem, vmem),
        scratch_shapes=[
            pltpu.VMEM((count, 2 * height, columns), jnp.bfloat16),
            pltpu.VMEM((count * 2 * height, wide), jnp.bfloat16),
            pltpu.VMEM((4 * TAPS * height, count * 2 * height), jnp.bfloat16),
            pltpu.VMEM((owners, rows, LANES), jnp.float32),
            pltpu.VMEM((count, rows, LANES), jnp.float32),
            pltpu.VMEM((owners, rows, LANES), jnp.float32),
            dma((count // 2,)), dma((count // 2,)), dma((count,)),
            dma((owners,)), dma((count,)), dma((count,)), dma((owners,)),
        ],
        compiler_params=pltpu.CompilerParams(collective_id=0, has_side_effects=True),
    )(signal, weight, shifts, phases)


def solution(mesh):
    part = P(("groups", "vel"), None, None)
    own = P("vel", None, None)
    return jax.shard_map(
        functools.partial(body, mesh.shape["vel"]),
        mesh=mesh,
        in_specs=(part, part, own, own),
        out_specs=(part, P("groups", None)),
        check_vma=False,
    )
```

```python
import functools
import math

import jax
import jax.numpy as jnp
import numpy as np
from jax import lax
from jax.experimental import pallas as pl
from jax.experimental.pallas import tpu as pltpu
from jax.sharding import PartitionSpec as P

TAPS = 6
PHASES = 8
LANES = 128
MESH = pl.DeviceIdType.MESH


def tap_table():
    distance = (np.arange(TAPS)[None, :] - 2) - np.arange(PHASES)[:, None] / 8.0
    raw = np.sinc(distance) * np.sinc(distance / 3.0)
    return (raw / raw.sum(axis=1, keepdims=True)).astype(np.float32)


def loop(start, stop, step):
    if stop - start <= 16:
        for at in range(start, stop):
            step(at)
    else:
        lax.fori_loop(start, stop, lambda at, c: (step(at), c)[1], 0)


def pick_phase(phase, column):
    value = jnp.full(phase.shape, float(column[0]), jnp.float32)
    for at in range(1, PHASES):
        value = jnp.where(phase == at, float(column[at]), value)
    return value


def coefficient_rows(shifts_ref, phases_ref, exposures, height):
    depth = exposures * 2 * height
    table = tap_table()
    lane = lax.broadcasted_iota(jnp.int32, (1, depth), 1)
    owner = lane // (2 * height)

    def spread(e, held):
        row_shift, row_phase, col_phase = held
        here = owner == e
        return (
            jnp.where(here, shifts_ref[0, 0, e], row_shift),
            jnp.where(here, phases_ref[0, 0, e], row_phase),
            jnp.where(here, phases_ref[0, 1, e], col_phase),
        )

    held = (jnp.zeros((1, depth), jnp.int32),) * 3
    if exposures <= 16:
        for e in range(exposures):
            held = spread(e, held)
    else:
        held = lax.fori_loop(0, exposures, spread, held)
    row_shift, row_phase, col_phase = held
    row_out = lax.broadcasted_iota(jnp.int32, (height, depth), 0)
    tap_index = lane % height - row_out + 2 - row_shift
    row_taps = jnp.zeros((height, depth), jnp.float32)
    for k in range(TAPS):
        row_taps = jnp.where(tap_index == k, pick_phase(row_phase, table[:, k]), row_taps)
    col_taps = [pick_phase(col_phase, table[:, k]) for k in range(TAPS)]
    image = (lane // height) % 2
    rows = []
    for which in range(2):
        masked = jnp.where(image == which, row_taps, 0.0)
        rows += [masked * col_taps[k] for k in range(TAPS)]
    full = jnp.concatenate(rows, axis=0)
    high = full.astype(jnp.bfloat16)
    low = (full - high.astype(jnp.float32)).astype(jnp.bfloat16)
    return jnp.concatenate([high, low], axis=0)


def kernel(
    count, height, columns, wide,
    signal_hbm, weight_hbm, shifts_hbm, phases_hbm, lik_hbm, best_hbm,
    own, shifts_ref, phases_ref, images, moved, coefs, lik, halves, pair_in, gathered, best,
    send_a, send_f, recv_a, send_g, recv_g, pair_sem, last_sem, load_sem, store_sem,
):
    me = lax.axis_index("vel")
    core = lax.rem(me, 2)
    chip = me // 2
    chips = count // 2
    partner = me + 1 - 2 * core
    half = columns // 2

    loads = [
        pltpu.make_async_copy(signal_hbm.at[0], own.at[0], load_sem.at[0]),
        pltpu.make_async_copy(weight_hbm.at[0], own.at[1], load_sem.at[1]),
        pltpu.make_async_copy(shifts_hbm, shifts_ref, load_sem.at[2]),
        pltpu.make_async_copy(phases_hbm, phases_ref, load_sem.at[3]),
    ]
    for copy in loads:
        copy.start()

    def source(d, side):
        return lax.rem(chip + chips - d, chips) * 2 + side

    def target(d):
        return lax.rem(chip + d, chips) * 2 + core

    barrier = pltpu.get_barrier_semaphore()

    def greet(to):
        pl.semaphore_signal(barrier, inc=1, device_id={"vel": to}, device_id_type=MESH)

    loop(1, chips, lambda d: greet(target(d)))
    greet(partner)
    for copy in loads:
        copy.wait()
    images[me] = jnp.concatenate(
        [own[0].astype(jnp.float32), own[1].astype(jnp.float32)], axis=0
    ).astype(jnp.bfloat16)
    coefs[...] = coefficient_rows(shifts_ref, phases_ref, count, height)
    pl.semaphore_wait(barrier, chips)

    def block_copy(e, to, send_sem):
        return pltpu.make_async_remote_copy(
            src_ref=images.at[e], dst_ref=images.at[e], send_sem=send_sem,
            recv_sem=recv_a.at[e], device_id={"vel": to}, device_id_type=MESH,
        )

    def place(e):
        block = images[e].astype(jnp.float32)
        block = jnp.concatenate(
            [block, jnp.zeros((2 * height, wide - columns), jnp.float32)], axis=1
        )
        amount = lax.rem(wide + 2 - shifts_ref[0, 1, e], wide)
        start = pl.multiple_of(e * 2 * height, 2 * height)
        moved[pl.ds(start, 2 * height), :] = pltpu.roll(block, amount, 1).astype(jnp.bfloat16)

    loop(1, chips, lambda d: block_copy(me, target(d), send_a.at[d]).start())
    block_copy(me, partner, send_f.at[0]).start()
    place(me)

    def relay(d):
        e = source(d, core)
        block_copy(e, partner, send_f.at[d]).wait_recv()
        block_copy(e, partner, send_f.at[d]).start()
        place(e)

    loop(1, chips, relay)

    def arrive(d):
        e = source(d, 1 - core)
        block_copy(e, partner, send_f.at[d]).wait_recv()
        place(e)

    loop(0, chips, arrive)

    acc = jnp.dot(coefs[...], moved[...], preferred_element_type=jnp.float32)
    size = 2 * TAPS * height
    acc = acc[:size] + acc[size:]
    sums = []
    for which in range(2):
        total = None
        for k in range(TAPS):
            at = (which * TAPS + k) * height
            term = acc[at : at + height]
            if k:
                term = pltpu.roll(term, wide - k, 1)
            term = term[:, :columns]
            total = term if total is None else total + term
        sums.append(total)
    likelihood = sums[0] / jnp.sqrt(jnp.maximum(sums[1], 1.0))
    halves[0] = likelihood[:, :half]
    halves[1] = likelihood[:, half:]
    lik[...] = likelihood

    def pair_copy(src, dst, sems):
        return pltpu.make_async_remote_copy(
            src_ref=src, dst_ref=dst, send_sem=sems.at[0], recv_sem=sems.at[1],
            device_id={"vel": partner}, device_id_type=MESH,
        )

    exchange = pair_copy(halves.at[1 - core], pair_in, pair_sem)
    exchange.start()
    store_lik = pltpu.make_async_copy(lik, lik_hbm.at[0], store_sem.at[0])
    store_lik.start()
    exchange.wait_recv()
    gathered[chip] = jnp.maximum(halves[core], pair_in[...])

    def gather_copy(slot, to, d):
        return pltpu.make_async_remote_copy(
            src_ref=gathered.at[slot], dst_ref=gathered.at[slot], send_sem=send_g.at[d],
            recv_sem=recv_g.at[slot], device_id={"vel": to}, device_id_type=MESH,
        )

    loop(1, chips, lambda d: gather_copy(chip, target(d), d).start())
    loop(1, chips, lambda d: gather_copy(source(d, 0) // 2, partner, d).wait_recv())
    best[core] = jnp.max(gathered[...], axis=0)
    share = pair_copy(best.at[core], best.at[core], last_sem)
    share.start()
    share.wait_recv()
    stores = [
        pltpu.make_async_copy(
            best.at[side], best_hbm.at[:, side * half : (side + 1) * half], store_sem.at[1 + side]
        )
        for side in range(2)
    ]
    for copy in stores:
        copy.start()
    loop(1, chips, lambda d: block_copy(me, target(d), send_a.at[d]).wait_send())
    loop(0, chips, lambda d: block_copy(source(d, core), partner, send_f.at[d]).wait_send())
    loop(1, chips, lambda d: gather_copy(chip, target(d), d).wait_send())
    exchange.wait_send()
    share.wait_send()
    store_lik.wait()
    for copy in stores:
        copy.wait()


def body(count, signal, weight, shifts, phases):
    height, columns = signal.shape[1], signal.shape[2]
    exposures = shifts.shape[1]
    reach = exposures + 5
    wide = columns + -(-reach // LANES) * LANES
    half = columns // 2
    chips = count // 2
    dma = pltpu.SemaphoreType.DMA
    hbm = pl.BlockSpec(memory_space=pl.ANY)
    return pl.pallas_call(
        functools.partial(kernel, count, height, columns, wide),
        out_shape=(
            jax.ShapeDtypeStruct((1, height, columns), jnp.float32),
            jax.ShapeDtypeStruct((height, columns), jnp.float32),
        ),
        in_specs=[hbm] * 4,
        out_specs=(hbm, hbm),
        scratch_shapes=[
            pltpu.VMEM((2, height, columns), jnp.bfloat16),
            pltpu.SMEM((1, 2, exposures), jnp.int32),
            pltpu.SMEM((1, 2, exposures), jnp.int32),
            pltpu.VMEM((count, 2 * height, columns), jnp.bfloat16),
            pltpu.VMEM((count * 2 * height, wide), jnp.bfloat16),
            pltpu.VMEM((4 * TAPS * height, count * 2 * height), jnp.bfloat16),
            pltpu.VMEM((height, columns), jnp.float32),
            pltpu.VMEM((2, height, half), jnp.float32),
            pltpu.VMEM((height, half), jnp.float32),
            pltpu.VMEM((chips, height, half), jnp.float32),
            pltpu.VMEM((2, height, half), jnp.float32),
            dma((chips,)), dma((chips,)), dma((count,)),
            dma((chips,)), dma((chips,)), dma((2,)), dma((2,)), dma((4,)), dma((3,)),
        ],
        compiler_params=pltpu.CompilerParams(collective_id=0, has_side_effects=True),
    )(signal, weight, jnp.swapaxes(shifts, 1, 2), jnp.swapaxes(phases, 1, 2))


def solution(mesh):
    part = P(("groups", "vel"), None, None)
    own = P("vel", None, None)
    return jax.shard_map(
        functools.partial(body, mesh.shape["vel"]),
        mesh=mesh,
        in_specs=(part, part, own, own),
        out_specs=(part, P("groups", None)),
        check_vma=False,
    )
```
